512 devices in a mesh: ctx: 64 (over z, x, core), tp: 8 (over y).
Axes of the slice: x: 4, y: 8, z: 8, core: 2. Of those that a mesh axis runs over, the one named last changes fastest.
Arguments:
- queries: bfloat16 [16384, 8192], P('ctx', 'tp'), may hold values from -8 to 8
- key_heads: bfloat16 [16384, 1024], P('ctx', 'tp'), may hold values from -8 to 8
- value_heads: bfloat16 [16384, 1024], P('ctx', 'tp'), may hold values from -6 to 6
- out_grad: bfloat16 [16384, 8192], P(('ctx', 'tp')), may hold values from -6 to 6
- doc_lengths: int32 [32], replicated, may hold values from 1 to 9, 128 in all
Outputs:
- grad_queries: bfloat16 [16384, 8192], P('ctx', 'tp')
- grad_keys: bfloat16 [16384, 1024], P('ctx', 'tp')
- grad_values: bfloat16 [16384, 1024], P('ctx', 'tp')
The draws below stay inside these ranges and needn't reach their ends.
Inputs may be any that keep to these rules, and one draw needn't show every extreme that they name: `doc_lengths`: documents fill the window in order, whole blocks of 128 rows each; the lengths sum to 128 and the longest is exactly 9.
All inputs are finite; a program needn't handle non-finite values.
Results may differ from the reference program's by a relative error of at most 0.009.
Values may be sent and summed in bfloat16 or wider, within the bound.
A program may use at most 64 MiB of HBM per device.

```python
import math
import jax
import jax.numpy as jnp
import numpy as np
from jax import lax

HD = 128
QH = 64
KVH = 8
GROUP = 8
BLK = 128
TOKENS = 16384
NBLK = 128
MAXDOC = 9
NDOCS = 32


def draw_queries(key, part):
    base = jnp.clip(jax.random.normal(jax.random.fold_in(key, 1), (TOKENS, QH * HD), jnp.float32), -6.0, 6.0)
    return base.astype(jnp.bfloat16)


def draw_key_heads(key, part):
    base = jnp.clip(jax.random.normal(jax.random.fold_in(key, 2), (TOKENS, KVH * HD), jnp.float32), -6.0, 6.0)
    return base.astype(jnp.bfloat16)


def levels(rng, shape, shards, low, largest):
    gain, own = 1.0, jax.random.fold_in(rng, 6)
    for axis_at, shards_of in shards:
        heights = jnp.exp(jax.random.uniform(jax.random.fold_in(own, axis_at), (shards_of,), jnp.float32, low / len(shards), largest / len(shards)))
        gain = gain * jnp.repeat(heights, shape[axis_at] // shards_of).reshape([-1 if axis == axis_at else 1 for axis in range(len(shape))])
    return gain


def split_up(amount, total, bound, lean):
    portions = [(1 << 20) // math.isqrt(standing ** lean) + 1 for standing in range(2, amount + 1)]
    rest, given = total - bound - (amount - 1), [1] * (amount - 1)
    while rest > 0:
        free = [i for i in range(amount - 1) if given[i] < bound]
        pool, remaining = sum([portions[i] for i in free]), rest
        for i in free:
            more = min(bound - given[i], max(1, remaining * portions[i] // pool), rest)
            given[i] = given[i] + more
            rest = rest - more
    return np.array([bound] + given)


def uneven(key, amount, total, limit, slope):
    if amount == 2:
        one = jax.random.randint(key, (), max(1, total - limit), min(limit, total - 1) + 1)
        return jnp.stack([one, total - one])
    tallies = jnp.asarray(split_up(amount, total, limit, slope), jnp.int32)
    couples = (amount - 1) // 2
    donor, taker = tallies[1:1 + 2 * couples:2], tallies[2:2 + 2 * couples:2]
    slack = jnp.minimum(donor - 1, limit - taker)
    moved = jax.random.randint(jax.random.fold_in(key, 1), (couples,), 0, 1 << 20) % (slack + 1)
    tallies = tallies.at[1:1 + 2 * couples:2].set(donor - moved).at[2:2 + 2 * couples:2].set(taker + moved)
    return tallies[jax.random.permutation(jax.random.fold_in(key, 2), amount)]


def centred(own_key, extent, scale, reach, pieces=(), kind=jnp.bfloat16):
    array = scale * jax.random.normal(own_key, extent, jnp.float32)
    if pieces:
        array = array * levels(own_key, extent, pieces, -0.22, 0.18)
    return jnp.clip(array, -reach, reach).astype(kind)


def setup_inputs(seed: int = 0) -> dict:
    key_of = jax.random.split(jax.random.key(seed), 6)
    queries = draw_queries(jax.random.fold_in(key_of[5], 71), 0)
    key_heads = draw_key_heads(jax.random.fold_in(key_of[5], 71), 0)
    value_heads = centred(key_of[2], (TOKENS, KVH * HD), 1.0, 6.0, ((0, 64), (1, 8)))
    out_grad = centred(key_of[3], (TOKENS, QH * HD), 1.0, 6.0, ((0, 512),))
    doc_lengths = uneven(key_of[4], NDOCS, NBLK, MAXDOC, 2).astype(jnp.int32)
    return {"queries": queries, "key_heads": key_heads, "value_heads": value_heads, "out_grad": out_grad, "doc_lengths": doc_lengths}


def doc_index(rows, doc_ends):
    return jnp.sum((rows[:, None] >= doc_ends[None, :]).astype(jnp.int32), axis=1)


def reference(queries, key_heads, value_heads, out_grad, doc_lengths):
    score_scale = HD ** -0.5
    window = MAXDOC * BLK
    behind = (MAXDOC - 1) * BLK
    doc_ends = jnp.cumsum(doc_lengths).astype(jnp.int32) * BLK
    padding = jnp.zeros((behind, KVH * HD), jnp.bfloat16)
    keys_pad = jnp.concatenate([padding, key_heads], axis=0)
    values_pad = jnp.concatenate([padding, value_heads], axis=0)
    offsets = jnp.arange(BLK, dtype=jnp.int32)
    spread = jnp.arange(window, dtype=jnp.int32)
    highest = lax.Precision.HIGHEST

    def block_step(state, block_id):
        grad_k, grad_v = state
        start_row = (block_id * BLK).astype(jnp.int32)
        query_rows = start_row + offsets
        key_rows = start_row - behind + spread
        allowed = (doc_index(query_rows, doc_ends)[:, None] == doc_index(key_rows, doc_ends)[None, :]) & (key_rows[None, :] <= query_rows[:, None]) & (key_rows[None, :] >= 0)
        query_block = lax.dynamic_slice_in_dim(queries, start_row, BLK, 0).astype(jnp.float32).reshape(BLK, KVH, GROUP, HD)
        grad_block = lax.dynamic_slice_in_dim(out_grad, start_row, BLK, 0).astype(jnp.float32).reshape(BLK, KVH, GROUP, HD)
        key_block = lax.dynamic_slice_in_dim(keys_pad, start_row, window, 0).astype(jnp.float32).reshape(window, KVH, HD)
        value_block = lax.dynamic_slice_in_dim(values_pad, start_row, window, 0).astype(jnp.float32).reshape(window, KVH, HD)
        scores = jnp.einsum("rkgd,ckd->kgrc", query_block, key_block, precision=highest)
        scores = jnp.where(allowed, scores * score_scale, -jnp.inf)
        row_max = jnp.max(scores, axis=-1)
        row_sum = jnp.sum(jnp.exp(scores - row_max[..., None]), axis=-1)
        log_total = row_max + jnp.log(row_sum)
        weights = jnp.exp(scores - log_total[..., None])
        grad_prob = jnp.einsum("rkgd,ckd->kgrc", grad_block, value_block, precision=highest)
        grad_dot = jnp.sum(weights * grad_prob, axis=-1)
        rounded = lax.optimization_barrier(weights.astype(jnp.bfloat16)).astype(jnp.float32)
        value_term = jnp.einsum("kgrc,rkgd->ckd", rounded, grad_block, precision=highest).reshape(window, KVH * HD)
        dscore = lax.optimization_barrier((weights * (grad_prob - grad_dot[..., None])).astype(jnp.bfloat16)).astype(jnp.float32)
        query_term = jnp.einsum("kgrc,ckd->rkgd", dscore, key_block, precision=highest) * score_scale
        key_term = jnp.einsum("kgrc,rkgd->ckd", dscore, query_block, precision=highest).reshape(window, KVH * HD) * score_scale
        grad_k = lax.dynamic_update_slice_in_dim(grad_k, lax.dynamic_slice_in_dim(grad_k, start_row, window, 0) + key_term, start_row, 0)
        grad_v = lax.dynamic_update_slice_in_dim(grad_v, lax.dynamic_slice_in_dim(grad_v, start_row, window, 0) + value_term, start_row, 0)
        return (grad_k, grad_v), query_term.reshape(BLK, QH * HD).astype(jnp.bfloat16)

    zero_pad = jnp.zeros((TOKENS + behind, KVH * HD), jnp.float32)
    (grad_k, grad_v), grad_q = lax.scan(block_step, (zero_pad, zero_pad), jnp.arange(NBLK, dtype=jnp.int32))
    return (grad_q.reshape(TOKENS, QH * HD), grad_k[behind:].astype(jnp.bfloat16), grad_v[behind:].astype(jnp.bfloat16))
```

```python
import functools

import jax
import jax.numpy as jnp
from jax import lax
from jax.experimental import pallas as pl
from jax.experimental.pallas import tpu as pltpu
from jax.sharding import PartitionSpec as P

HD = 128
GROUP = 8
BLK = 128
REACH = 4
ROWS = 256
CHUNKS = REACH + 1
BIG = 1e30
FLOOR = -1e29
SCALE = HD ** (-0.5)
LOG2E = 1.4426950408889634
MESH = pl.DeviceIdType.MESH
NT = (((1,), (1,)), ((), ()))
NN = (((1,), (0,)), ((), ()))


def mm(a, b, dims):
    return lax.dot_general(a, b, dims, preferred_element_type=jnp.float32)


def kernel(n_ctx, n_tp, lengths, queries, key_heads, value_heads, out_grad, dq_out, dk_out, dv_out,
           q, keys, values, keys_t, grads, probs, dprobs, top, total, factor, hide, dkey, dvalue, dq,
           send_k, send_v, got_k, got_v, own_k, own_v,
           q_sem, kv_own_sem, k_recv, v_recv, kv_send, g_recv, g_send, c_send, ck_recv, cv_recv, dq_sem, out_sem):
    i = lax.axis_index("ctx")
    t = lax.axis_index("tp")

    def q_copy(h):
        return pltpu.make_async_copy(queries.at[:, pl.ds(h * HD, HD)], q.at[h], q_sem)

    for h in range(GROUP):
        q_copy(h).start()
    k_own = pltpu.make_async_copy(key_heads, keys.at[pl.ds(REACH * ROWS, ROWS)], kv_own_sem.at[0])
    v_own = pltpu.make_async_copy(value_heads, values.at[pl.ds(REACH * ROWS, ROWS)], kv_own_sem.at[1])
    k_own.start()
    v_own.start()

    barrier = pltpu.get_barrier_semaphore()
    for d in range(1, n_tp):
        pl.semaphore_signal(barrier, inc=1, device_id={"tp": lax.rem(t + d, n_tp)}, device_id_type=MESH)
    for d in range(1, REACH + 1):
        @pl.when(i >= d)
        def _():
            pl.semaphore_signal(barrier, inc=1, device_id={"ctx": i - d}, device_id_type=MESH)

        @pl.when(i + d < n_ctx)
        def _():
            pl.semaphore_signal(barrier, inc=1, device_id={"ctx": i + d}, device_id_type=MESH)

    def scan_doc(k, carry):
        end, first0, first1 = carry
        end = end + lengths[k]
        first0 = jnp.where(end <= 2 * i, jnp.maximum(first0, end), first0)
        first1 = jnp.where(end <= 2 * i + 1, jnp.maximum(first1, end), first1)
        return end, first0, first1

    _, first0, first1 = lax.fori_loop(0, lengths.shape[0], scan_doc, (jnp.int32(0), jnp.int32(0), jnp.int32(0)))
    lane = lax.broadcasted_iota(jnp.int32, (1, ROWS), 1)
    first = jnp.where(lane < BLK, first0, first1)
    last = jnp.where(lane < BLK, 2 * i, 2 * i + 1)
    for j in range(2 * CHUNKS):
        block = 2 * i - 2 * REACH + j
        hide[pl.ds(j, 1), :] = jnp.where((block >= first) & (block <= last), 0.0, BIG)
    for j in range(REACH):
        @pl.when(i < REACH - j)
        def _():
            keys[pl.ds(j * ROWS, ROWS), :] = jnp.zeros((ROWS, HD), jnp.bfloat16)
            values[pl.ds(j * ROWS, ROWS), :] = jnp.zeros((ROWS, HD), jnp.bfloat16)
    dkey[...] = jnp.zeros_like(dkey)
    dvalue[...] = jnp.zeros_like(dvalue)

    partners = n_tp - 1 + jnp.minimum(i, REACH) + jnp.minimum(n_ctx - 1 - i, REACH)
    pl.semaphore_wait(barrier, partners)

    def kv_copy(d, what):
        src, dst, recv = ((key_heads, keys, k_recv), (value_heads, values, v_recv))[what]
        return pltpu.make_async_remote_copy(
            src_ref=src, dst_ref=dst.at[pl.ds((REACH - d) * ROWS, ROWS)], send_sem=kv_send.at[d - 1, what],
            recv_sem=recv.at[REACH - d], device_id={"ctx": i + d}, device_id_type=MESH)

    def kv_start(what):
        for d in range(1, REACH + 1):
            @pl.when(i + d < n_ctx)
            def _():
                kv_copy(d, what).start()

    def grad_copy(h, peer):
        return pltpu.make_async_remote_copy(
            src_ref=out_grad.at[:, pl.ds(pl.multiple_of(peer * (GROUP * HD) + h * HD, HD), HD)],
            dst_ref=grads.at[h, pl.ds(t * (ROWS // n_tp), ROWS // n_tp)],
            send_sem=g_send, recv_sem=g_recv.at[h], device_id={"tp": peer}, device_id_type=MESH)

    def grad_start(h):
        for d in (4, 3, 5, 2, 6, 1, 7):
            grad_copy(h, lax.rem(t + d, n_tp)).start()
        pltpu.make_async_copy(
            out_grad.at[:, pl.ds(pl.multiple_of(t * (GROUP * HD) + h * HD, HD), HD)],
            grads.at[h, pl.ds(t * (ROWS // n_tp), ROWS // n_tp)], g_recv.at[h]).start()

    kv_start(0)
    grad_start(0)
    grad_start(1)
    kv_start(1)

    def grads_on(h, carry):
        grad_start(h)
        return carry

    lax.fori_loop(2, GROUP, grads_on, 0)

    pltpu.make_async_copy(q, q, q_sem).wait()
    k_own.wait()

    def scores(j, own):
        rows = pl.ds(j * ROWS, ROWS) if own else pl.ds(pl.multiple_of(j * ROWS, ROWS), ROWS)
        key = keys[rows, :]
        keys_t[j] = key.T
        hide0, hide1 = hide[pl.ds(2 * j, 1), :], hide[pl.ds(2 * j + 1, 1), :]

        def head(h, carry):
            raw = mm(key, q[h], NT) * (SCALE * LOG2E)
            if own:
                row_k = lax.broadcasted_iota(jnp.int32, (ROWS, ROWS), 0)
                row_q = lax.broadcasted_iota(jnp.int32, (ROWS, ROWS), 1)
                raw = jnp.where(row_k <= row_q, raw, -BIG)
            high0 = jnp.max(raw[:BLK], axis=0, keepdims=True) - hide0
            high1 = jnp.max(raw[BLK:], axis=0, keepdims=True) - hide1
            high = jnp.maximum(jnp.maximum(high0, high1), FLOOR)
            e0 = jnp.exp2(raw[:BLK] - (high + hide0))
            e1 = jnp.exp2(raw[BLK:] - (high + hide1))
            top[j, pl.ds(h, 1), :] = high
            total[j, pl.ds(h, 1), :] = jnp.sum(e0, axis=0, keepdims=True) + jnp.sum(e1, axis=0, keepdims=True)
            probs[h, j, :BLK, :] = e0.astype(jnp.bfloat16)
            probs[h, j, BLK:, :] = e1.astype(jnp.bfloat16)
            return carry

        lax.fori_loop(0, GROUP, head, 0)

    scores(REACH, True)

    def far(step, carry):
        j = REACH - 1 - step

        @pl.when(i >= REACH - j)
        def _():
            at = keys.at[pl.ds(pl.multiple_of(j * ROWS, ROWS), ROWS)]
            pltpu.make_async_copy(at, at, k_recv.at[j]).wait()

        scores(j, False)
        return carry

    lax.fori_loop(0, REACH, far, 0)

    highest = jnp.max(top[...], axis=0)
    lifted = [jnp.exp2(top[j] - highest) for j in range(CHUNKS)]
    inverse = 1.0 / sum(lifted[j] * total[j] for j in range(CHUNKS))
    for j in range(CHUNKS):
        factor[j] = lifted[j] * inverse

    v_own.wait()
    for j in range(REACH):
        @pl.when(i >= REACH - j)
        def _():
            at = values.at[pl.ds(j * ROWS, ROWS)]
            pltpu.make_async_copy(at, at, v_recv.at[j]).wait()

    def backward(h, carry):
        pltpu.make_async_copy(grads.at[h], grads.at[h], g_recv.at[h]).wait()
        grad = grads[h]
        query = q[h]
        dots = jnp.zeros((1, ROWS), jnp.float32)
        for j in range(CHUNKS):
            dp = mm(values[pl.ds(j * ROWS, ROWS), :], grad, NT)
            p = probs[h, j].astype(jnp.float32) * factor[j, pl.ds(h, 1), :]
            dots = dots + jnp.sum(p * dp, axis=0, keepdims=True)
            dprobs[j] = dp
            pb = p.astype(jnp.bfloat16)
            probs[h, j] = pb
            rows = pl.ds(j * ROWS, ROWS)
            dvalue[rows, :] += mm(pb, grad, NN)
        dq_t = jnp.zeros((HD, ROWS), jnp.float32)
        for j in range(CHUNKS):
            rows = pl.ds(j * ROWS, ROWS)
            ds = (probs[h, j].astype(jnp.float32) * (dprobs[j] - dots)).astype(jnp.bfloat16)
            dkey[rows, :] += mm(ds, query, NN)
            dq_t = dq_t + mm(keys_t[j], ds, NN)
        dq[h] = (dq_t.T * SCALE).astype(jnp.bfloat16)
        return carry

    lax.fori_loop(0, GROUP, backward, 0)

    def part_copy(d, what):
        src, dst, recv = ((send_k, got_k, ck_recv), (send_v, got_v, cv_recv))[what]
        return pltpu.make_async_remote_copy(
            src_ref=src.at[d - 1], dst_ref=dst.at[d - 1], send_sem=c_send.at[d - 1, what],
            recv_sem=recv.at[d - 1], device_id={"ctx": i - d}, device_id_type=MESH)

    for d in range(REACH, 0, -1):
        rows = pl.ds((REACH - d) * ROWS, ROWS)
        send_k[d - 1] = (dkey[rows, :] * SCALE).astype(jnp.bfloat16)
        send_v[d - 1] = dvalue[rows, :].astype(jnp.bfloat16)

        @pl.when(i >= d)
        def _():
            part_copy(d, 0).start()
            part_copy(d, 1).start()

    for h in range(GROUP):
        pltpu.make_async_copy(dq.at[h], dq_out.at[:, pl.ds(h * HD, HD)], dq_sem).start()

    rows = pl.ds(REACH * ROWS, ROWS)
    dkey[rows, :] = dkey[rows, :] * SCALE
    for d in range(1, REACH + 1):
        @pl.when(i + d < n_ctx)
        def _():
            part_copy(d, 0).wait_recv()
            dkey[rows, :] += got_k[d - 1].astype(jnp.float32)
            part_copy(d, 1).wait_recv()
            dvalue[rows, :] += got_v[d - 1].astype(jnp.float32)
    own_k[...] = dkey[rows, :].astype(jnp.bfloat16)
    own_v[...] = dvalue[rows, :].astype(jnp.bfloat16)
    k_back = pltpu.make_async_copy(own_k, dk_out, out_sem.at[0])
    v_back = pltpu.make_async_copy(own_v, dv_out, out_sem.at[1])
    k_back.start()
    v_back.start()

    for d in range(1, REACH + 1):
        @pl.when(i + d < n_ctx)
        def _():
            kv_copy(d, 0).wait_send()
            kv_copy(d, 1).wait_send()

        @pl.when(i >= d)
        def _():
            part_copy(d, 0).wait_send()
            part_copy(d, 1).wait_send()
    sent = grads.at[pl.ds(0, n_tp - 1)]
    pltpu.make_async_copy(sent, sent, g_send).wait()
    pltpu.make_async_copy(dq, dq, dq_sem).wait()
    k_back.wait()
    v_back.wait()


def body(n_ctx, n_tp, queries, key_heads, value_heads, out_grad, doc_lengths):
    bf, f32 = jnp.bfloat16, jnp.float32
    any_space = pl.BlockSpec(memory_space=pl.ANY)
    dma = pltpu.SemaphoreType.DMA
    return pl.pallas_call(
        functools.partial(kernel, n_ctx, n_tp),
        out_shape=(jax.ShapeDtypeStruct(queries.shape, bf), jax.ShapeDtypeStruct(key_heads.shape, bf),
                   jax.ShapeDtypeStruct(value_heads.shape, bf)),
        in_specs=[pl.BlockSpec(memory_space=pltpu.SMEM)] + [any_space] * 4,
        out_specs=[any_space] * 3,
        scratch_shapes=[
            pltpu.VMEM((GROUP, ROWS, HD), bf),
            pltpu.VMEM((CHUNKS * ROWS, HD), bf),
            pltpu.VMEM((CHUNKS * ROWS, HD), bf),
            pltpu.VMEM((CHUNKS, HD, ROWS), bf),
            pltpu.VMEM((GROUP, ROWS, HD), bf),
            pltpu.VMEM((GROUP, CHUNKS, ROWS, ROWS), bf),
            pltpu.VMEM((CHUNKS, ROWS, ROWS), f32),
            pltpu.VMEM((CHUNKS, GROUP, ROWS), f32),
            pltpu.VMEM((CHUNKS, GROUP, ROWS), f32),
            pltpu.VMEM((CHUNKS, GROUP, ROWS), f32),
            pltpu.VMEM((16, ROWS), f32),
            pltpu.VMEM((CHUNKS * ROWS, HD), f32),
            pltpu.VMEM((CHUNKS * ROWS, HD), f32),
            pltpu.VMEM((GROUP, ROWS, HD), bf),
            pltpu.VMEM((REACH, ROWS, HD), bf),
            pltpu.VMEM((REACH, ROWS, HD), bf),
            pltpu.VMEM((REACH, ROWS, HD), bf),
            pltpu.VMEM((REACH, ROWS, HD), bf),
            pltpu.VMEM((ROWS, HD), bf),
            pltpu.VMEM((ROWS, HD), bf),
            dma, dma((2,)), dma((REACH,)), dma((REACH,)), dma((REACH, 2)), dma((GROUP,)), dma, dma((REACH, 2)),
            dma((REACH,)), dma((REACH,)), dma, dma((2,)),
        ],
        compiler_params=pltpu.CompilerParams(collective_id=0, has_side_effects=True, vmem_limit_bytes=56 << 20),
    )(doc_lengths, queries, key_heads, value_heads, out_grad)


def solution(mesh):
    placed = (P("ctx", "tp"), P("ctx", "tp"), P("ctx", "tp"), P(("ctx", "tp"), None), P())
    return jax.shard_map(
        functools.partial(body, mesh.shape["ctx"], mesh.shape["tp"]),
        mesh=mesh,
        in_specs=placed,
        out_specs=(P("ctx", "tp"), P("ctx", "tp"), P("ctx", "tp")),
        check_vma=False,
    )
```

```python
import functools

import jax
import jax.numpy as jnp
from jax import lax
from jax.experimental import pallas as pl
from jax.experimental.pallas import tpu as pltpu
from jax.sharding import PartitionSpec as P

HD = 128
GROUP = 8
BLK = 128
REACH = 4
ROWS = 256
CHUNKS = REACH + 1
BATCH = 4
BIG = 1e30
FLOOR = -1e29
SCALE = HD ** (-0.5)
MESH = pl.DeviceIdType.MESH
NT = (((1,), (1,)), ((), ()))
NN = (((1,), (0,)), ((), ()))


def mm(a, b, dims=NN):
    return lax.dot_general(a, b, dims, preferred_element_type=jnp.float32)


def block(j):
    return pl.ds(j * ROWS if isinstance(j, int) else pl.multiple_of(j * ROWS, ROWS), ROWS)


def kernel(n_ctx, n_tp, lengths, queries, key_heads, value_heads, out_grad, dq, dkv,
           q, keys, values, keys_t, values_t, grads, probs, outs, top, total, factor, hide, dkey, dvalue,
           swap, swapped, part, got, q_sem, own_sem, k_recv, v_recv, kv_send, fwd_send, g_recv, g_send,
           swap_send, swap_recv, part_send, part_recv):
    i = lax.axis_index("ctx")
    t = lax.axis_index("tp")
    odd = lax.rem(i, 2)
    even = odd == 0
    partner = i + 1 - 2 * odd

    for h in range(GROUP):
        pltpu.make_async_copy(queries.at[:, pl.ds(h * HD, HD)], q.at[h], q_sem).start()
    k_own = pltpu.make_async_copy(key_heads, keys.at[block(REACH)], own_sem.at[0])
    v_own = pltpu.make_async_copy(value_heads, values.at[block(REACH)], own_sem.at[1])
    k_own.start()
    v_own.start()

    barrier = pltpu.get_barrier_semaphore()
    for d in range(1, n_tp):
        pl.semaphore_signal(barrier, inc=1, device_id={"tp": lax.rem(t + d, n_tp)}, device_id_type=MESH)
    pl.semaphore_signal(barrier, inc=1, device_id={"ctx": partner}, device_id_type=MESH)
    for d in (2, 4):
        @pl.when(i >= d)
        def _():
            pl.semaphore_signal(barrier, inc=1, device_id={"ctx": i - d}, device_id_type=MESH)

        @pl.when(i + d < n_ctx)
        def _():
            pl.semaphore_signal(barrier, inc=1, device_id={"ctx": i + d}, device_id_type=MESH)

    def scan_doc(k, carry):
        end, first0, first1 = carry
        end = end + lengths[k]
        first0 = jnp.where(end <= 2 * i, jnp.maximum(first0, end), first0)
        first1 = jnp.where(end <= 2 * i + 1, jnp.maximum(first1, end), first1)
        return end, first0, first1

    _, first0, first1 = lax.fori_loop(0, lengths.shape[0], scan_doc, (jnp.int32(0), jnp.int32(0), jnp.int32(0)))
    lane = lax.broadcasted_iota(jnp.int32, (1, ROWS), 1)
    first = jnp.where(lane < BLK, first0, first1)
    last = jnp.where(lane < BLK, 2 * i, 2 * i + 1)
    for j in range(2 * CHUNKS):
        at = 2 * i - 2 * REACH + j
        hide[pl.ds(j, 1), :] = jnp.where((at >= first) & (at <= last), 0.0, BIG)
    for d in range(1, REACH + 1):
        @pl.when(i < d)
        def _():
            keys[block(REACH - d), :] = jnp.zeros((ROWS, HD), jnp.bfloat16)
            values[block(REACH - d), :] = jnp.zeros((ROWS, HD), jnp.bfloat16)
    dkey[...] = jnp.zeros_like(dkey)
    dvalue[...] = jnp.zeros_like(dvalue)

    partners = n_tp
    for d in (2, 4):
        partners = partners + jnp.where(i >= d, 1, 0) + jnp.where(i + d < n_ctx, 1, 0)
    pl.semaphore_wait(barrier, partners)

    def own_copy(d, what):
        src, dst, recv = ((key_heads, keys, k_recv), (value_heads, values, v_recv))[what]
        return pltpu.make_async_remote_copy(
            src_ref=src, dst_ref=dst.at[block(REACH - d)], send_sem=kv_send.at[d // 2, what],
            recv_sem=recv.at[REACH - d], device_id={"ctx": i + d}, device_id_type=MESH)

    def own_start(what):
        for d in (2, 4):
            @pl.when(i + d < n_ctx)
            def _():
                own_copy(d, what).start()

        @pl.when(even)
        def _():
            own_copy(1, what).start()

    def forward(d, to, what):
        ref, recv = ((keys, k_recv), (values, v_recv))[what]
        return pltpu.make_async_remote_copy(
            src_ref=ref.at[block(REACH - d)], dst_ref=ref.at[block(REACH - to)], send_sem=fwd_send.at[d // 2 - 1, what],
            recv_sem=recv.at[REACH - to], device_id={"ctx": partner}, device_id_type=MESH)

    def arrived(d, what):
        ref, recv = ((keys, k_recv), (values, v_recv))[what]

        @pl.when(i >= d)
        def _():
            at = ref.at[block(REACH - d)]
            pltpu.make_async_copy(at, at, recv.at[REACH - d]).wait()

    def pass_on(d, what):
        arrived(d, what)
        if d == 2:
            @pl.when((i >= d) & even)
            def _():
                forward(2, 3, what).start()

            @pl.when((i >= d) & (odd == 1))
            def _():
                forward(2, 1, what).start()
        else:
            @pl.when((i >= d) & (odd == 1))
            def _():
                forward(4, 3, what).start()

    def grad_copy(h, peer):
        return pltpu.make_async_remote_copy(
            src_ref=out_grad.at[:, pl.ds(pl.multiple_of(peer * (GROUP * HD) + h * HD, HD), HD)],
            dst_ref=grads.at[h, pl.ds(t * (ROWS // n_tp), ROWS // n_tp)],
            send_sem=g_send, recv_sem=g_recv.at[h], device_id={"tp": peer}, device_id_type=MESH)

    def grad_start(h, carry):
        for d in (4, 3, 5, 2, 6, 1, 7):
            grad_copy(h, lax.rem(t + d, n_tp)).start()
        pltpu.make_async_copy(
            out_grad.at[:, pl.ds(pl.multiple_of(t * (GROUP * HD) + h * HD, HD), HD)],
            grads.at[h, pl.ds(t * (ROWS // n_tp), ROWS // n_tp)], g_recv.at[h]).start()
        return carry

    own_start(0)
    lax.fori_loop(0, 2, grad_start, 0)
    own_start(1)
    lax.fori_loop(2, GROUP, grad_start, 0)

    pltpu.make_async_copy(q, q, q_sem).wait()
    k_own.wait()

    def scores(j, own):
        key = keys[block(j), :]
        keys_t[j] = key.T
        hide0, hide1 = hide[pl.ds(2 * j, 1), :], hide[pl.ds(2 * j + 1, 1), :]

        def some(batch, carry):
            for x in range(BATCH):
                h = batch * BATCH + x
                raw = mm(key, q[h], NT) * SCALE
                if own:
                    row_k = lax.broadcasted_iota(jnp.int32, (ROWS, ROWS), 0)
                    row_q = lax.broadcasted_iota(jnp.int32, (ROWS, ROWS), 1)
                    raw = jnp.where(row_k <= row_q, raw, -BIG)
                high0 = jnp.max(raw[:BLK], axis=0, keepdims=True) - hide0
                high1 = jnp.max(raw[BLK:], axis=0, keepdims=True) - hide1
                high = jnp.maximum(jnp.maximum(high0, high1), FLOOR)
                e0 = jnp.exp(raw[:BLK] - (high + hide0))
                e1 = jnp.exp(raw[BLK:] - (high + hide1))
                top[j, pl.ds(h, 1), :] = high
                total[j, pl.ds(h, 1), :] = jnp.sum(e0, axis=0, keepdims=True) + jnp.sum(e1, axis=0, keepdims=True)
                probs[j, :BLK, block(h)] = e0.astype(jnp.bfloat16)
                probs[j, BLK:, block(h)] = e1.astype(jnp.bfloat16)
            return carry

        lax.fori_loop(0, GROUP // BATCH, some, 0)

    scores(REACH, True)

    def far(step, carry):
        d = jnp.where(step < 2, 2 * step + 2, 2 * step - 3)
        for s, (d_k, d_v) in enumerate(((2, 0), (4, 0), (1, 2), (3, 4))):
            @pl.when(step == s)
            def _():
                pass_on(d_k, 0) if s < 2 else arrived(d_k, 0)
                if d_v:
                    pass_on(d_v, 1)
        scores(REACH - d, False)
        return carry

    lax.fori_loop(0, REACH, far, 0)

    highest = jnp.max(top[...], axis=0)
    lifted = [jnp.exp(top[j] - highest) for j in range(CHUNKS)]
    inverse = 1.0 / sum(lifted[j] * total[j] for j in range(CHUNKS))
    for j in range(CHUNKS):
        factor[j] = lifted[j] * inverse

    v_own.wait()
    arrived(1, 1)
    arrived(3, 1)
    for j in range(CHUNKS):
        values_t[j] = values[block(j), :].T

    def weigh(batch, carry):
        for x in range(2):
            h = batch * 2 + x
            out_t = jnp.zeros((HD, ROWS), jnp.float32)
            for j in range(CHUNKS):
                p = (probs[j, :, block(h)].astype(jnp.float32) * factor[j, pl.ds(h, 1), :]).astype(jnp.bfloat16)
                probs[j, :, block(h)] = p
                out_t = out_t + mm(values_t[j], p)
            outs[h] = out_t
        return carry

    lax.fori_loop(0, GROUP // 2, weigh, 0)

    def backward(pair, carry):
        heads = [2 * pair, 2 * pair + 1]
        for h in heads:
            pltpu.make_async_copy(grads.at[h], grads.at[h], g_recv.at[h]).wait()
        both = pl.ds(pl.multiple_of(pair * 2 * ROWS, 2 * ROWS), 2 * ROWS)
        grad_rows = grads[pl.ds(2 * pair, 2)].reshape(2 * ROWS, HD)
        query_rows = q[pl.ds(2 * pair, 2)].reshape(2 * ROWS, HD)
        grads_t = [grads[h].T for h in heads]
        dots = [jnp.sum(outs[h] * grads_t[x].astype(jnp.float32), axis=0, keepdims=True) for x, h in enumerate(heads)]
        dq_t = [jnp.zeros((HD, ROWS), jnp.float32) for _ in heads]
        for j in range(CHUNKS):
            ds = []
            for x, h in enumerate(heads):
                dp = mm(values[block(j), :], grads_t[x])
                ds.append(probs[j, :, block(h)] * (dp - dots[x]).astype(jnp.bfloat16))
                dq_t[x] = dq_t[x] + mm(keys_t[j], ds[x])
            dvalue[block(j), :] += mm(probs[j, :, both], grad_rows)
            dkey[block(j), :] += mm(jnp.concatenate(ds, axis=1), query_rows)
        for x, h in enumerate(heads):
            dq[:, pl.ds(pl.multiple_of(h * HD, HD), HD)] = (dq_t[x].T * SCALE).astype(jnp.bfloat16)
        return carry

    lax.fori_loop(0, GROUP // 2, backward, 0)

    def swap_copy(s):
        return pltpu.make_async_remote_copy(
            src_ref=swap.at[s], dst_ref=swapped.at[s], send_sem=swap_send.at[s], recv_sem=swap_recv.at[s],
            device_id={"ctx": partner}, device_id_type=MESH)

    def part_copy(s):
        return pltpu.make_async_remote_copy(
            src_ref=part.at[s], dst_ref=got.at[s], send_sem=part_send.at[s], recv_sem=part_recv.at[s],
            device_id={"ctx": i - 2 * (s + 1)}, device_id_type=MESH)

    def send_part(s, other):
        rows = block(REACH - 2 * (s + 1))
        key_sum, value_sum = dkey[rows, :] * SCALE, dvalue[rows, :]
        if other is not None:
            key_sum = key_sum + swapped[other, 0].astype(jnp.float32)
            value_sum = value_sum + swapped[other, 1].astype(jnp.float32)
        part[s, 0] = key_sum.astype(jnp.bfloat16)
        part[s, 1] = value_sum.astype(jnp.bfloat16)

        @pl.when(i >= 2 * (s + 1))
        def _():
            part_copy(s).start()

    for s in (1, 0):
        rows = block(REACH - (2 * s + 1))
        swap[s, 0] = (dkey[rows, :] * SCALE).astype(jnp.bfloat16)
        swap[s, 1] = dvalue[rows, :].astype(jnp.bfloat16)
        swap_copy(s).start()

    own = block(REACH)
    dkey[own, :] = dkey[own, :] * SCALE

    @pl.when(even)
    def _():
        send_part(1, None)
        swap_copy(1).wait_recv()
        send_part(0, 1)
        swap_copy(0).wait_recv()
        dkey[own, :] += swapped[0, 0].astype(jnp.float32)
        dvalue[own, :] += swapped[0, 1].astype(jnp.float32)

    @pl.when(odd == 1)
    def _():
        swap_copy(1).wait_recv()
        send_part(1, 1)
        swap_copy(0).wait_recv()
        send_part(0, 0)

    for s in (0, 1):
        @pl.when(i + 2 * (s + 1) < n_ctx)
        def _():
            part_copy(s).wait_recv()
            dkey[own, :] += got[s, 0].astype(jnp.float32)
            dvalue[own, :] += got[s, 1].astype(jnp.float32)
    dkv[0] = dkey[own, :].astype(jnp.bfloat16)
    dkv[1] = dvalue[own, :].astype(jnp.bfloat16)

    for s in (0, 1):
        swap_copy(s).wait_send()

        @pl.when(i >= 2 * (s + 1))
        def _():
            part_copy(s).wait_send()

    for what in (0, 1):
        for d in (2, 4):
            @pl.when(i + d < n_ctx)
            def _():
                own_copy(d, what).wait_send()

        @pl.when(even)
        def _():
            own_copy(1, what).wait_send()

        @pl.when(i >= 2)
        def _():
            forward(2, 1, what).wait_send()

        @pl.when((i >= 4) & (odd == 1))
        def _():
            forward(4, 3, what).wait_send()
    sent = grads.at[pl.ds(0, n_tp - 1)]
    pltpu.make_async_copy(sent, sent, g_send).wait()


def put_out(dq, dkv, dq_out, dk_out, dv_out, sems):
    copies = [pltpu.make_async_copy(dq, dq_out, sems.at[0]), pltpu.make_async_copy(dkv.at[0], dk_out, sems.at[1]),
              pltpu.make_async_copy(dkv.at[1], dv_out, sems.at[2])]
    for copy in copies:
        copy.start()
    for copy in copies:
        copy.wait()


def body(n_ctx, n_tp, queries, key_heads, value_heads, out_grad, doc_lengths):
    bf, f32 = jnp.bfloat16, jnp.float32
    any_space = pl.BlockSpec(memory_space=pl.ANY)
    vmem = pl.BlockSpec(memory_space=pltpu.VMEM)
    dma = pltpu.SemaphoreType.DMA
    dq, dkv = pl.pallas_call(
        functools.partial(kernel, n_ctx, n_tp),
        out_shape=(pltpu.VMEM((ROWS, GROUP * HD), bf), pltpu.VMEM((2, ROWS, HD), bf)),
        in_specs=[pl.BlockSpec(memory_space=pltpu.SMEM)] + [any_space] * 4,
        out_specs=[vmem] * 2,
        scratch_shapes=[
            pltpu.VMEM((GROUP, ROWS, HD), bf),
            pltpu.VMEM((CHUNKS * ROWS, HD), bf),
            pltpu.VMEM((CHUNKS * ROWS, HD), bf),
            pltpu.VMEM((CHUNKS, HD, ROWS), bf),
            pltpu.VMEM((CHUNKS, HD, ROWS), bf),
            pltpu.VMEM((GROUP, ROWS, HD), bf),
            pltpu.VMEM((CHUNKS, ROWS, GROUP * ROWS), bf),
            pltpu.VMEM((GROUP, HD, ROWS), f32),
            pltpu.VMEM((CHUNKS, GROUP, ROWS), f32),
            pltpu.VMEM((CHUNKS, GROUP, ROWS), f32),
            pltpu.VMEM((CHUNKS, GROUP, ROWS), f32),
            pltpu.VMEM((16, ROWS), f32),
            pltpu.VMEM((CHUNKS * ROWS, HD), f32),
            pltpu.VMEM((CHUNKS * ROWS, HD), f32),
            pltpu.VMEM((2, 2, ROWS, HD), bf),
            pltpu.VMEM((2, 2, ROWS, HD), bf),
            pltpu.VMEM((2, 2, ROWS, HD), bf),
            pltpu.VMEM((2, 2, ROWS, HD), bf),
            dma, dma((2,)), dma((REACH,)), dma((REACH,)), dma((3, 2)), dma((2, 2)), dma((GROUP,)), dma,
            dma((2,)), dma((2,)), dma((2,)), dma((2,)),
        ],
        compiler_params=pltpu.CompilerParams(collective_id=0, has_side_effects=True, vmem_limit_bytes=56 << 20),
    )(doc_lengths, queries, key_heads, value_heads, out_grad)
    return pl.pallas_call(
        put_out,
        out_shape=(jax.ShapeDtypeStruct(queries.shape, bf), jax.ShapeDtypeStruct(key_heads.shape, bf),
                   jax.ShapeDtypeStruct(value_heads.shape, bf)),
        in_specs=[vmem] * 2,
        out_specs=[any_space] * 3,
        scratch_shapes=[dma((3,))],
    )(pltpu.with_memory_space_constraint(dq, pltpu.VMEM), pltpu.with_memory_space_constraint(dkv, pltpu.VMEM))


def solution(mesh):
    placed = (P("ctx", "tp"), P("ctx", "tp"), P("ctx", "tp"), P(("ctx", "tp"), None), P())
    return jax.shard_map(
        functools.partial(body, mesh.shape["ctx"], mesh.shape["tp"]),
        mesh=mesh,
        in_specs=placed,
        out_specs=(P("ctx", "tp"), P("ctx", "tp"), P("ctx", "tp")),
        check_vma=False,
    )
```
